128 devices in a mesh: cache: 32 (over y, z, core), cand: 4 (over x).
Axes of the slice: x: 4, y: 4, z: 4, core: 2. Of those that a mesh axis runs over, the one named last changes fastest.
Arguments:
- cand_states: bfloat16 [1024, 64, 1024], P('cand', 'cache'), may hold values from -6 to 6
- in_proj: bfloat16 [1024, 4, 1024], P(None, None, 'cand'), may hold values from -0.1875 to 0.1875
- out_proj: bfloat16 [1024, 1024], P('cand'), may hold values from -0.1875 to 0.1875
- history: bfloat16 [32, 64, 2, 128, 1024], P('cache', None, None, None, 'cand'), may hold values from -6 to 6
- lengths: int32 [64], replicated, may hold values from 2048 to 4096, as said below
- rank_users: int32 [64], replicated, may hold values from 0 to 63, each once
- recency_bias: float32 [8, 14], P('cand'), may hold values from -4 to 4
- score_weight: float32 [1024], replicated, may hold values from -0.1875 to 0.1875
Outputs:
- layer_out: bfloat16 [1024, 64, 1024], P('cand', 'cache')
- scores: float32 [1024, 64], P('cand', 'cache')
The draws below stay inside these ranges and needn't reach their ends.
Inputs may be any that keep to these rules, and one draw needn't show every extreme that they name: `lengths`: every length is a multiple of 128; some user's length is exactly 4096. `rank_users`: each user is ranked in exactly one slot.
All inputs are finite; a program needn't handle non-finite values.
Results may differ from the reference program's by a relative error of at most 0.008.
Values may be sent and summed in bfloat16 or wider, within the bound.
A program may use at most 128 MiB of HBM per device.

```python
import jax
import jax.numpy as jnp
from jax import lax

D = 1024
HEADS = 8
HD = 128
BLOCK = 128
BUCKETS = 14
H_MAX = 4096
SHARDS = 32
USERS = 64
CANDS = 1024
PAGE_EV = 128


def draw_lengths(key, part):
    blocks_max = H_MAX // BLOCK
    counts = jax.random.randint(jax.random.fold_in(key, 11), (USERS,), blocks_max // 2, blocks_max + 1)
    longest = jax.random.randint(jax.random.fold_in(key, 12), (), 0, USERS)
    counts = jnp.where(jnp.arange(USERS) == longest, blocks_max, counts)
    return (counts * BLOCK).astype(jnp.int32)


def level_of(own_key, shape, cuts, least, top_value):
    factor_of, own = 1.0, jax.random.fold_in(own_key, 6)
    for dim, parts in cuts:
        steps = jnp.exp(jax.random.uniform(jax.random.fold_in(own, dim), (parts,), jnp.float32, least / len(cuts), top_value / len(cuts)))
        factor_of = factor_of * jnp.repeat(steps, shape[dim] // parts).reshape([-1 if axis == dim else 1 for axis in range(len(shape))])
    return factor_of


def scatter_about(rng, extent, scale, most, pieces=(), held_as=jnp.bfloat16):
    drawn = jax.random.normal(rng, extent, jnp.float32) * scale
    if len(pieces) > 0:
        drawn = level_of(rng, extent, pieces, -0.22, 0.18) * drawn
    return jnp.clip(drawn, min=-most, max=most).astype(held_as)


def setup_inputs(seed: int = 0) -> dict:
    key_of = jax.random.split(jax.random.key(seed), 9)
    cand_states = scatter_about(key_of[0], (CANDS, USERS, D), 1.0, 6.0, ((0, 4), (1, 32)))
    in_proj = scatter_about(key_of[1], (D, 4, D), D ** -0.5, 0.1875, ((2, 4),))
    out_proj = scatter_about(key_of[2], (D, D), D ** -0.5, 0.1875, ((0, 4),))
    history = scatter_about(key_of[3], (SHARDS, USERS, 2, PAGE_EV, D), 1.0, 6.0, ((0, 32), (4, 4)))
    lengths = draw_lengths(jax.random.fold_in(key_of[8], 71), 0)
    rank_users = jax.random.permutation(key_of[5], USERS).astype(jnp.int32)
    recency_bias = scatter_about(key_of[6], (HEADS, BUCKETS), 1.0, 4.0, ((0, 4),), jnp.float32)
    score_weight = scatter_about(key_of[7], (D,), D ** -0.5, 0.1875, (), jnp.float32)
    return {"cand_states": cand_states, "in_proj": in_proj, "out_proj": out_proj, "history": history, "lengths": lengths, "rank_users": rank_users, "recency_bias": recency_bias, "score_weight": score_weight}


EPSILON = 1e-06

def bucket_index(distance, bucket_count):
    powers = 2 ** jnp.arange(bucket_count - 1, dtype=jnp.int32)
    return lax.optimization_barrier(jnp.sum((distance[..., None] >= powers).astype(jnp.int32), axis=-1)).astype(jnp.int32)

def reference(cand_states, in_proj, out_proj, history, lengths, rank_users, recency_bias, score_weight):
    float_states = cand_states.astype(jnp.float32)
    normed = (float_states * lax.rsqrt(lax.optimization_barrier(jnp.mean(float_states * float_states, axis=-1, keepdims=True)) + EPSILON)).astype(jnp.bfloat16)
    projected = jnp.dot(normed.reshape(CANDS * USERS, D), in_proj.reshape(D, 4 * D), preferred_element_type=jnp.float32)
    projected = jax.nn.silu(projected).astype(jnp.bfloat16).reshape(CANDS, USERS, 4, D)
    scale = HD ** (-0.5)
    cache_ids = jnp.arange(SHARDS, dtype=jnp.int32)[:, None]
    event_ids = jnp.arange(PAGE_EV, dtype=jnp.int32)[None, :]

    def attend_user(slot_index):
        user = rank_users[slot_index].astype(jnp.int32)
        length = lengths[user]
        stored = lax.dynamic_index_in_dim(history, user, 1, keepdims=False)
        hist_keys = stored[:, 0].reshape(H_MAX, HEADS, HD).astype(jnp.float32)
        hist_values = stored[:, 1].reshape(H_MAX, HEADS, HD).astype(jnp.float32)
        block_ids = event_ids // BLOCK * SHARDS + jnp.remainder(cache_ids - user, SHARDS)
        positions = (block_ids * BLOCK + event_ids % BLOCK).reshape(H_MAX)
        usable = positions < length
        distance = jnp.maximum(length - positions, 0)
        bias_table = recency_bias[:, bucket_index(distance, BUCKETS)]
        own = lax.dynamic_index_in_dim(projected, slot_index, 1, keepdims=False).astype(jnp.float32)
        gates = own[:, 0].reshape(CANDS, HEADS, HD)
        own_values = own[:, 1].reshape(CANDS, HEADS, HD)
        queries = own[:, 2].reshape(CANDS, HEADS, HD)
        own_keys = own[:, 3].reshape(CANDS, HEADS, HD)
        scores = jnp.einsum('chd,khd->chk', queries, hist_keys) * scale + bias_table[None]
        weights = jnp.where(usable[None, None, :], jax.nn.silu(scores), 0.0).astype(jnp.bfloat16)
        weights = lax.optimization_barrier(weights).astype(jnp.float32)
        totals = jnp.einsum('chk,khd->chd', weights, hist_values)
        self_scores = lax.optimization_barrier(jnp.sum(queries * own_keys, axis=-1)) * scale + recency_bias[:, 0][None, :]
        totals = totals + jax.nn.silu(self_scores)[..., None] * own_values
        normalized = totals * lax.rsqrt(lax.optimization_barrier(jnp.mean(totals * totals, axis=-1, keepdims=True)) + EPSILON)
        return (normalized * gates).astype(jnp.bfloat16).reshape(CANDS, D)
    gated = lax.map(attend_user, jnp.arange(USERS, dtype=jnp.int32))
    gated = jnp.transpose(gated, (1, 0, 2))
    branch = jnp.dot(gated.reshape(CANDS * USERS, D), out_proj, preferred_element_type=jnp.float32).reshape(CANDS, USERS, D)
    layer_sum = float_states + branch
    scores_out = lax.optimization_barrier(jnp.sum(layer_sum * score_weight, axis=-1))
    return (layer_sum.astype(jnp.bfloat16), scores_out)
```

```python
import functools

import jax
import jax.numpy as jnp
from jax import lax
from jax.experimental import pallas as pl
from jax.experimental.pallas import tpu as pltpu
from jax.sharding import PartitionSpec as P

EPSILON = 1e-06
MESH = pl.DeviceIdType.MESH
BF16, F32 = jnp.bfloat16, jnp.float32

X = 4
SIDE = 4
CACHE = 2 * SIDE * SIDE
MEMBERS = 2
HEADS_HERE, HD = 2, 128
HW = HEADS_HERE * HD
ROWS = 256
D = 1024
EV = 128
GROUPS, IN_GROUP = 8, 4
BUCKETS = 14
MASKED = -1e30


def silu(x):
    half = x * 0.5
    return half + half * jnp.tanh(half)


def kernel(
    lengths_ref,
    users_ref,
    recency_ref,
    weight_ref,
    cand_hbm,
    win_hbm,
    wout_hbm,
    hist_hbm,
    out_ref,
    scores_ref,
    hist_v,
    send_v,
    arr_v,
    cand_v,
    norm_v,
    win_v,
    wout_v,
    proj_v,
    tot_v,
    gated_v,
    spread_v,
    bias_v,
    local_sem,
    hist_ss,
    hist_rs,
    norm_ss,
    norm_rs,
    wout_ss,
    wout_rs,
    gate_ss,
    gate_rs,
):
    me, mx = lax.axis_index("cache"), lax.axis_index("cand")
    my_y, my_z, my_core = me // (2 * SIDE), (me // 2) % SIDE, me % 2
    scale = HD ** (-0.5)

    def cache_at(group, b, sign):
        a, dc = group // 2, group % 2
        ny = (my_y + sign * b + SIDE) % SIDE
        nz = (my_z + sign * ((a + b) % SIDE) + SIDE) % SIDE
        nc = (my_core + dc) % 2
        return (ny * SIDE + nz) * 2 + nc

    def hist_copy(m, group, b, kv):
        slot = group * IN_GROUP + b
        return pltpu.make_async_remote_copy(
            src_ref=send_v.at[m, slot, kv],
            dst_ref=arr_v.at[m, slot, kv],
            send_sem=hist_ss.at[m, slot, kv],
            recv_sem=hist_rs.at[m, slot, kv],
            device_id={"cache": cache_at(group, b, 1), "cand": mx},
            device_id_type=MESH,
        )

    def norm_copy(m, d):
        return pltpu.make_async_remote_copy(
            src_ref=norm_v.at[m, mx],
            dst_ref=norm_v.at[m, mx],
            send_sem=norm_ss.at[m, d],
            recv_sem=norm_rs.at[m, d],
            device_id={"cache": me, "cand": (mx + d) % X},
            device_id_type=MESH,
        )

    def wout_copy(d):
        return pltpu.make_async_remote_copy(
            src_ref=wout_v.at[mx],
            dst_ref=wout_v.at[mx],
            send_sem=wout_ss.at[d],
            recv_sem=wout_rs.at[d],
            device_id={"cache": me, "cand": (mx + d) % X},
            device_id_type=MESH,
        )

    def gate_copy(m, d):
        return pltpu.make_async_remote_copy(
            src_ref=gated_v.at[m, (mx + d) % X],
            dst_ref=spread_v.at[m, mx],
            send_sem=gate_ss.at[m, d],
            recv_sem=gate_rs.at[m, d],
            device_id={"cache": me, "cand": (mx + d) % X},
            device_id_type=MESH,
        )

    cand_in = pltpu.make_async_copy(cand_hbm, cand_v, local_sem.at[0])
    hist_in = pltpu.make_async_copy(hist_hbm, hist_v, local_sem.at[1])
    win_in = pltpu.make_async_copy(win_hbm, win_v, local_sem.at[2])
    wout_in = pltpu.make_async_copy(wout_hbm, wout_v.at[mx], local_sem.at[3])
    cand_in.start()
    hist_in.start()
    win_in.start()
    wout_in.start()

    barrier = pltpu.get_barrier_semaphore()

    def greet(j, _):
        pl.semaphore_signal(
            barrier,
            inc=1,
            device_id={"cache": (me + j) % CACHE, "cand": mx},
            device_id_type=MESH,
        )
        return 0

    lax.fori_loop(1, CACHE, greet, 0)
    for d in range(1, X):
        pl.semaphore_signal(
            barrier, inc=1, device_id={"cache": me, "cand": (mx + d) % X}, device_id_type=MESH
        )

    cand_in.wait()
    TILE = 32

    def normalize(i, _):
        m, r = i // (ROWS // TILE), i % (ROWS // TILE)
        rows = pl.ds(pl.multiple_of(r * TILE, TILE), TILE)
        x = cand_v[m, rows, :].astype(F32)
        inv = lax.rsqrt(jnp.mean(x * x, axis=-1, keepdims=True) + EPSILON)
        norm_v[m, mx, rows, :] = (x * inv).astype(BF16)
        return 0

    lax.fori_loop(0, MEMBERS * (ROWS // TILE), normalize, 0)
    pl.semaphore_wait(barrier, CACHE - 1 + X - 1)
    for d in (2, 1, 3):
        norm_copy(0, d).start()
    hist_in.wait()

    def gather(m, group):
        for b in range(IN_GROUP):
            user = users_ref[MEMBERS * cache_at(group, b, 1) + m]
            block = hist_v[user]
            slot = group * IN_GROUP + b
            if b == 0:
                own = group == 0

                @pl.when(own)
                def _():
                    arr_v[m, slot] = block

                @pl.when(jnp.logical_not(own))
                def _():
                    send_v[m, slot] = block
            else:
                send_v[m, slot] = block

    def send(m, group):
        for kv in range(2):
            for b in range(IN_GROUP):
                if b == 0:

                    @pl.when(group > 0)
                    def _():
                        hist_copy(m, group, b, kv).start()
                else:
                    hist_copy(m, group, b, kv).start()

    for m in range(MEMBERS):
        gather(m, 0)

        def gather_and_send(group, _):
            @pl.when(group < GROUPS - 1)
            def _():
                gather(m, group + 1)

            send(m, group)
            return 0

        lax.fori_loop(0, GROUPS, gather_and_send, 0)
        if m == 0:
            for d in (2, 1, 3):
                norm_copy(1, d).start()
            wout_in.wait()
            for d in (2, 1, 3):
                wout_copy(d).start()

    lanes = lax.broadcasted_iota(jnp.int32, (1, EV), 1)

    def bias_of(i, _):
        m, group = i // GROUPS, i % GROUPS
        user = users_ref[MEMBERS * me + m]
        length = lengths_ref[user]
        for b in range(IN_GROUP):
            shard = cache_at(group, b, -1)
            position = lax.rem(shard - user + 4 * CACHE, CACHE) * EV + lanes
            distance = jnp.maximum(length - position, 0)
            usable = position < length
            for h in range(HEADS_HERE):
                bias = jnp.full((1, EV), recency_ref[h, 0], F32)
                for k in range(BUCKETS - 1):
                    bias = jnp.where(distance >= 2**k, recency_ref[h, k + 1], bias)
                bias = jnp.where(usable, bias * 0.5, MASKED)
                bias_v[m, h, group, :, b * EV : (b + 1) * EV] = bias
        return 0

    lax.fori_loop(0, MEMBERS * GROUPS, bias_of, 0)
    win_in.wait()

    def project(m):
        def from_source(d, _):
            @pl.when(d > 0)
            def _():
                norm_copy(m, d).wait_recv()

            source = (mx - d + X) % X

            def one_kind(kind, _):
                columns = pl.ds(pl.multiple_of(kind * HW, HW), HW)
                product = jnp.dot(
                    norm_v[m, source], win_v[:, columns], preferred_element_type=F32
                )
                rows = pl.ds(pl.multiple_of(source * ROWS, ROWS), ROWS)
                proj_v[m, kind, rows, :] = silu(product).astype(BF16)
                return 0

            lax.fori_loop(0, 4, one_kind, 0)
            return 0

        lax.fori_loop(0, X, from_source, 0)

        def own_term(t, _):
            rows = pl.ds(pl.multiple_of(t * ROWS, ROWS), ROWS)
            for h in range(HEADS_HERE):
                cols = slice(h * HD, (h + 1) * HD)
                values = proj_v[m, 1, rows, cols].astype(F32)
                queries = proj_v[m, 2, rows, cols].astype(F32)
                keys = proj_v[m, 3, rows, cols].astype(F32)
                score = jnp.sum(queries * keys, axis=-1, keepdims=True) * scale + recency_ref[h, 0]
                tot_v[m, h, rows, :] = silu(score) * values
            return 0

        lax.fori_loop(0, X, own_term, 0)

    def arrived(m, group):
        for b in range(IN_GROUP):
            for kv in range(2):
                if b == 0:

                    @pl.when(group > 0)
                    def _():
                        hist_copy(m, group, b, kv).wait_recv()
                else:
                    hist_copy(m, group, b, kv).wait_recv()

    def attend(m, group, t):
        rows = pl.ds(pl.multiple_of(t * ROWS, ROWS), ROWS)
        slots = pl.ds(group * IN_GROUP, IN_GROUP)
        for h in range(HEADS_HERE):
            cols = slice(h * HD, (h + 1) * HD)
            keys = arr_v[m, slots, 0, :, cols].reshape(IN_GROUP * EV, HD)
            values = arr_v[m, slots, 1, :, cols].reshape(IN_GROUP * EV, HD)
            scores = lax.dot_general(
                proj_v[m, 2, rows, cols],
                keys,
                (((1,), (1,)), ((), ())),
                preferred_element_type=F32,
            )
            half = scores * (0.5 * scale) + bias_v[m, h, group]
            weights = (half + half * jnp.tanh(half)).astype(BF16)
            tot_v[m, h, rows, :] += jnp.dot(weights, values, preferred_element_type=F32)

    def finish(m, d):
        t = (mx + d) % X
        rows = pl.ds(pl.multiple_of(t * ROWS, ROWS), ROWS)
        for h in range(HEADS_HERE):
            cols = slice(h * HD, (h + 1) * HD)
            total = tot_v[m, h, rows, :]
            inv = lax.rsqrt(jnp.mean(total * total, axis=-1, keepdims=True) + EPSILON)
            value = (total * inv * proj_v[m, 0, rows, cols].astype(F32)).astype(BF16)
            if d == 0:
                spread_v[m, mx, :, cols] = value
            else:
                gated_v[m, t, :, cols] = value
        if d != 0:
            gate_copy(m, d).start()

    def attend_groups(m, first, last):
        def step(group, _):
            arrived(m, group)

            def tile(t, _):
                attend(m, group, t)
                return 0

            lax.fori_loop(0, X, tile, 0)
            return 0

        lax.fori_loop(first, last, step, 0)

    def output(m):
        for d in range(1, X):
            gate_copy(m, d).wait_recv()
        partial = jnp.zeros((ROWS, HD), F32)
        wide = 256
        for c in range(D // wide):
            cols = slice(c * wide, (c + 1) * wide)
            total = cand_v[m, :, cols].astype(F32)
            for s in range(X):
                total += jnp.dot(spread_v[m, s], wout_v[s, :, cols], preferred_element_type=F32)
            out_ref[m, :, cols] = total.astype(BF16)
            weighted = total * weight_ref[:, cols]
            for k in range(wide // HD):
                partial += weighted[:, k * HD : (k + 1) * HD]
        scores_ref[m : m + 1, :] = jnp.sum(partial.T, axis=0, keepdims=True)

    project(0)
    attend_groups(0, 0, GROUPS)
    for d in (2, 1, 3, 0):
        finish(0, d)
    project(1)
    attend_groups(1, 0, GROUPS // 2)
    for d in range(1, X):
        wout_copy(d).wait_recv()
    output(0)
    attend_groups(1, GROUPS // 2, GROUPS - 1)
    arrived(1, GROUPS - 1)
    for d in (2, 1, 3, 0):
        attend(1, GROUPS - 1, (mx + d) % X)
        finish(1, d)

    def drain(i, _):
        m, group = i // GROUPS, i % GROUPS
        for b in range(IN_GROUP):
            for kv in range(2):
                if b == 0:

                    @pl.when(group > 0)
                    def _():
                        hist_copy(m, group, b, kv).wait_send()
                else:
                    hist_copy(m, group, b, kv).wait_send()
        return 0

    lax.fori_loop(0, MEMBERS * GROUPS, drain, 0)
    for d in range(1, X):
        norm_copy(0, d).wait_send()
        norm_copy(1, d).wait_send()
        wout_copy(d).wait_send()
        gate_copy(0, d).wait_send()
    output(1)
    for d in range(1, X):
        gate_copy(1, d).wait_send()


def local(cand_states, in_proj, out_proj, history, lengths, rank_users, recency_bias, score_weight):
    members_first = jnp.transpose(cand_states, (1, 0, 2))
    in_matrix = in_proj.reshape(D, 4 * HW)
    stored = history.reshape(history.shape[1:])
    smem = pl.BlockSpec(memory_space=pltpu.SMEM)
    vmem = pl.BlockSpec(memory_space=pltpu.VMEM)
    hbm = pl.BlockSpec(memory_space=pl.ANY)
    dma = pltpu.SemaphoreType.DMA
    out, scores = pl.pallas_call(
        kernel,
        out_shape=(
            jax.ShapeDtypeStruct((MEMBERS, ROWS, D), BF16),
            jax.ShapeDtypeStruct((MEMBERS, ROWS), F32),
        ),
        in_specs=[smem, smem, smem, vmem, hbm, hbm, hbm, hbm],
        out_specs=(vmem, vmem),
        scratch_shapes=[
            pltpu.VMEM(stored.shape, BF16),
            pltpu.VMEM((MEMBERS, CACHE, 2, EV, HW), BF16),
            pltpu.VMEM((MEMBERS, CACHE, 2, EV, HW), BF16),
            pltpu.VMEM((MEMBERS, ROWS, D), BF16),
            pltpu.VMEM((MEMBERS, X, ROWS, D), BF16),
            pltpu.VMEM((D, 4 * HW), BF16),
            pltpu.VMEM((X, HW, D), BF16),
            pltpu.VMEM((MEMBERS, 4, X * ROWS, HW), BF16),
            pltpu.VMEM((MEMBERS, HEADS_HERE, X * ROWS, HD), F32),
            pltpu.VMEM((MEMBERS, X, ROWS, HW), BF16),
            pltpu.VMEM((MEMBERS, X, ROWS, HW), BF16),
            pltpu.VMEM((MEMBERS, HEADS_HERE, GROUPS, 1, IN_GROUP * EV), F32),
            dma((4,)),
            dma((MEMBERS, CACHE, 2)),
            dma((MEMBERS, CACHE, 2)),
            dma((MEMBERS, X)),
            dma((MEMBERS, X)),
            dma((X,)),
            dma((X,)),
            dma((MEMBERS, X)),
            dma((MEMBERS, X)),
        ],
        compiler_params=pltpu.CompilerParams(
            collective_id=0, has_side_effects=True, vmem_limit_bytes=63 << 20
        ),
    )(
        lengths,
        rank_users,
        recency_bias,
        score_weight.reshape(1, D),
        members_first,
        in_matrix,
        out_proj,
        stored,
    )
    return jnp.transpose(out, (1, 0, 2)), scores.T


def solution(mesh):
    in_specs = (
        P("cand", "cache", None),
        P(None, None, "cand"),
        P("cand", None),
        P("cache", None, None, None, "cand"),
        P(),
        P(),
        P("cand", None),
        P(),
    )
    out_specs = (P("cand", "cache", None), P("cand", "cache"))
    return jax.shard_map(local, mesh=mesh, in_specs=in_specs, out_specs=out_specs, check_vma=False)
```

```python
import functools

import jax
import jax.numpy as jnp
from jax import lax
from jax.experimental import pallas as pl
from jax.experimental.pallas import tpu as pltpu
from jax.sharding import PartitionSpec as P

EPSILON = 1e-06
MESH = pl.DeviceIdType.MESH
BF16, F32 = jnp.bfloat16, jnp.float32

X = 4
SIDE = 4
CACHE = 2 * SIDE * SIDE
MEMBERS = 2
HEADS_HERE, HD = 2, 128
HW = HEADS_HERE * HD
ROWS = 256
D = 1024
EV = 128
GROUPS, IN_GROUP = 8, 4
BUCKETS = 14
AHEAD = 6
MASKED = -1e30


def silu(x):
    half = x * 0.5
    return half + half * jnp.tanh(half)


def kernel(
    lengths_ref,
    users_ref,
    recency_ref,
    weight_ref,
    cand_hbm,
    win_hbm,
    wout_hbm,
    hist_hbm,
    out_ref,
    scores_ref,
    hist_v,
    send_v,
    arr_v,
    cand_v,
    norm_v,
    win_v,
    wout_v,
    proj_v,
    tot_v,
    gated_v,
    spread_v,
    bias_v,
    local_sem,
    hist_ss,
    hist_rs,
    norm_ss,
    norm_rs,
    wout_ss,
    wout_rs,
    gate_ss,
    gate_rs,
):
    me, mx = lax.axis_index("cache"), lax.axis_index("cand")
    my_y, my_z, my_core = me // (2 * SIDE), (me // 2) % SIDE, me % 2
    scale = HD ** (-0.5)

    def cache_at(group, b, sign):
        a, dc = group // 2, group % 2
        ny = (my_y + sign * b + SIDE) % SIDE
        nz = (my_z + sign * ((a + b) % SIDE) + SIDE) % SIDE
        nc = (my_core + dc) % 2
        return (ny * SIDE + nz) * 2 + nc

    def hist_copy(m, group, b, kv):
        slot = group * IN_GROUP + b
        return pltpu.make_async_remote_copy(
            src_ref=send_v.at[m, slot, kv],
            dst_ref=arr_v.at[m, slot, kv],
            send_sem=hist_ss.at[m, slot, kv],
            recv_sem=hist_rs.at[m, slot, kv],
            device_id={"cache": cache_at(group, b, 1), "cand": mx},
            device_id_type=MESH,
        )

    def norm_copy(m, d):
        return pltpu.make_async_remote_copy(
            src_ref=norm_v.at[m, mx],
            dst_ref=norm_v.at[m, mx],
            send_sem=norm_ss.at[m, d],
            recv_sem=norm_rs.at[m, d],
            device_id={"cache": me, "cand": (mx + d) % X},
            device_id_type=MESH,
        )

    def wout_copy(d):
        return pltpu.make_async_remote_copy(
            src_ref=wout_v.at[mx],
            dst_ref=wout_v.at[mx],
            send_sem=wout_ss.at[d],
            recv_sem=wout_rs.at[d],
            device_id={"cache": me, "cand": (mx + d) % X},
            device_id_type=MESH,
        )

    def gate_copy(m, d):
        return pltpu.make_async_remote_copy(
            src_ref=gated_v.at[m, (mx + d) % X],
            dst_ref=spread_v.at[m, mx],
            send_sem=gate_ss.at[m, d],
            recv_sem=gate_rs.at[m, d],
            device_id={"cache": me, "cand": (mx + d) % X},
            device_id_type=MESH,
        )

    cand_in = pltpu.make_async_copy(cand_hbm, cand_v, local_sem.at[0])
    hist_in = pltpu.make_async_copy(hist_hbm, hist_v, local_sem.at[1])
    win_in = pltpu.make_async_copy(win_hbm, win_v, local_sem.at[2])
    wout_in = pltpu.make_async_copy(wout_hbm, wout_v.at[mx], local_sem.at[3])
    cand_in.start()
    hist_in.start()
    win_in.start()
    wout_in.start()

    barrier = pltpu.get_barrier_semaphore()

    def greet(j, _):
        pl.semaphore_signal(
            barrier,
            inc=1,
            device_id={"cache": (me + j) % CACHE, "cand": mx},
            device_id_type=MESH,
        )
        return 0

    lax.fori_loop(1, CACHE, greet, 0)
    for d in range(1, X):
        pl.semaphore_signal(
            barrier, inc=1, device_id={"cache": me, "cand": (mx + d) % X}, device_id_type=MESH
        )

    cand_in.wait()
    TILE = 32

    def normalize(i, _):
        m, r = i // (ROWS // TILE), i % (ROWS // TILE)
        rows = pl.ds(pl.multiple_of(r * TILE, TILE), TILE)
        x = cand_v[m, rows, :].astype(F32)
        inv = lax.rsqrt(jnp.mean(x * x, axis=-1, keepdims=True) + EPSILON)
        norm_v[m, mx, rows, :] = (x * inv).astype(BF16)
        return 0

    lax.fori_loop(0, MEMBERS * (ROWS // TILE), normalize, 0)
    pl.semaphore_wait(barrier, CACHE - 1 + X - 1)
    for d in (2, 1, 3):
        norm_copy(0, d).start()
    hist_in.wait()

    def gather(m, group):
        for b in range(IN_GROUP):
            user = users_ref[MEMBERS * cache_at(group, b, 1) + m]
            block = hist_v[user]
            slot = group * IN_GROUP + b
            if b == 0:
                own = group == 0

                @pl.when(own)
                def _():
                    arr_v[m, slot] = block

                @pl.when(jnp.logical_not(own))
                def _():
                    send_v[m, slot] = block
            else:
                send_v[m, slot] = block

    def send(m, group):
        for kv in range(2):
            for b in range(IN_GROUP):
                if b == 0:

                    @pl.when(group > 0)
                    def _():
                        hist_copy(m, group, b, kv).start()
                else:
                    hist_copy(m, group, b, kv).start()

    gather(0, 0)

    def gather_and_send(group, _):
        @pl.when(group < GROUPS - 1)
        def _():
            gather(0, group + 1)

        send(0, group)
        return 0

    lax.fori_loop(0, GROUPS, gather_and_send, 0)
    for d in (2, 1, 3):
        norm_copy(1, d).start()
    wout_in.wait()
    for d in (2, 1, 3):
        wout_copy(d).start()

    def gather_next(group, _):
        gather(1, group)
        return 0

    lax.fori_loop(0, GROUPS, gather_next, 0)

    lanes = lax.broadcasted_iota(jnp.int32, (1, EV), 1)

    def bias_of(i, _):
        m, group = i // GROUPS, i % GROUPS
        user = users_ref[MEMBERS * me + m]
        length = lengths_ref[user]
        for b in range(IN_GROUP):
            shard = cache_at(group, b, -1)
            position = lax.rem(shard - user + 4 * CACHE, CACHE) * EV + lanes
            distance = jnp.maximum(length - position, 0)
            usable = position < length
            for h in range(HEADS_HERE):
                bias = jnp.full((1, EV), recency_ref[h, 0], F32)
                for k in range(BUCKETS - 1):
                    bias = jnp.where(distance >= 2**k, recency_ref[h, k + 1], bias)
                bias = jnp.where(usable, bias * 0.5, MASKED)
                bias_v[m, h, group, :, b * EV : (b + 1) * EV] = bias
        return 0

    lax.fori_loop(0, MEMBERS * GROUPS, bias_of, 0)
    win_in.wait()

    def project(m):
        def from_source(d, _):
            @pl.when(d > 0)
            def _():
                norm_copy(m, d).wait_recv()

            source = (mx - d + X) % X

            def one_kind(kind, _):
                columns = pl.ds(pl.multiple_of(kind * HW, HW), HW)
                product = jnp.dot(
                    norm_v[m, source], win_v[:, columns], preferred_element_type=F32
                )
                rows = pl.ds(pl.multiple_of(source * ROWS, ROWS), ROWS)
                proj_v[m, kind, rows, :] = silu(product).astype(BF16)
                return 0

            lax.fori_loop(0, 4, one_kind, 0)
            return 0

        lax.fori_loop(0, X, from_source, 0)

        def own_term(t, _):
            rows = pl.ds(pl.multiple_of(t * ROWS, ROWS), ROWS)
            for h in range(HEADS_HERE):
                cols = slice(h * HD, (h + 1) * HD)
                values = proj_v[m, 1, rows, cols].astype(F32)
                queries = proj_v[m, 2, rows, cols].astype(F32)
                keys = proj_v[m, 3, rows, cols].astype(F32)
                score = jnp.sum(queries * keys, axis=-1, keepdims=True) * scale + recency_ref[h, 0]
                tot_v[m, h, rows, :] = silu(score) * values
            return 0

        lax.fori_loop(0, X, own_term, 0)

    def arrived(m, group):
        for b in range(IN_GROUP):
            for kv in range(2):
                if b == 0:

                    @pl.when(group > 0)
                    def _():
                        hist_copy(m, group, b, kv).wait_recv()
                else:
                    hist_copy(m, group, b, kv).wait_recv()

    def sent(m, group):
        for b in range(IN_GROUP):
            for kv in range(2):
                if b == 0:

                    @pl.when(group > 0)
                    def _():
                        hist_copy(m, group, b, kv).wait_send()
                else:
                    hist_copy(m, group, b, kv).wait_send()

    def attend(m, group, t):
        rows = pl.ds(pl.multiple_of(t * ROWS, ROWS), ROWS)
        slots = pl.ds(group * IN_GROUP, IN_GROUP)
        for h in range(HEADS_HERE):
            cols = slice(h * HD, (h + 1) * HD)
            keys = arr_v[m, slots, 0, :, cols].reshape(IN_GROUP * EV, HD)
            values = arr_v[m, slots, 1, :, cols].reshape(IN_GROUP * EV, HD)
            scores = lax.dot_general(
                proj_v[m, 2, rows, cols],
                keys,
                (((1,), (1,)), ((), ())),
                preferred_element_type=F32,
            )
            half = scores * (0.5 * scale) + bias_v[m, h, group]
            weights = (half + half * jnp.tanh(half)).astype(BF16)
            tot_v[m, h, rows, :] += jnp.dot(weights, values, preferred_element_type=F32)

    def finish(m, d):
        t = (mx + d) % X
        rows = pl.ds(pl.multiple_of(t * ROWS, ROWS), ROWS)
        for h in range(HEADS_HERE):
            cols = slice(h * HD, (h + 1) * HD)
            total = tot_v[m, h, rows, :]
            inv = lax.rsqrt(jnp.mean(total * total, axis=-1, keepdims=True) + EPSILON)
            value = (total * inv * proj_v[m, 0, rows, cols].astype(F32)).astype(BF16)
            if d == 0:
                spread_v[m, mx, :, cols] = value
            else:
                gated_v[m, t, :, cols] = value
        if d != 0:
            gate_copy(m, d).start()

    def attend_groups(m, first, last):
        def step(group, _):
            arrived(m, group)
            if m == 0:
                sent(0, group)

                @pl.when(group + AHEAD >= GROUPS)
                def _():
                    send(1, group + AHEAD - GROUPS)
            else:

                @pl.when(group + AHEAD < GROUPS)
                def _():
                    sent(1, group)
                    send(1, group + AHEAD)

            def tile(t, _):
                attend(m, group, t)
                return 0

            lax.fori_loop(0, X, tile, 0)
            return 0

        lax.fori_loop(first, last, step, 0)

    def output(m):
        for d in range(1, X):
            gate_copy(m, d).wait_recv()
        partial = jnp.zeros((ROWS, HD), F32)
        wide = 256
        for c in range(D // wide):
            cols = slice(c * wide, (c + 1) * wide)
            total = cand_v[m, :, cols].astype(F32)
            for s in range(X):
                total += jnp.dot(spread_v[m, s], wout_v[s, :, cols], preferred_element_type=F32)
            out_ref[m, :, cols] = total.astype(BF16)
            weighted = total * weight_ref[:, cols]
            for k in range(wide // HD):
                partial += weighted[:, k * HD : (k + 1) * HD]
        scores_ref[m : m + 1, :] = jnp.sum(partial.T, axis=0, keepdims=True)

    project(0)
    attend_groups(0, 0, GROUPS)
    for d in (2, 1, 3, 0):
        finish(0, d)
    project(1)
    attend_groups(1, 0, GROUPS // 2)
    for d in range(1, X):
        wout_copy(d).wait_recv()
    output(0)
    attend_groups(1, GROUPS // 2, GROUPS - 1)
    arrived(1, GROUPS - 1)
    for d in (2, 1, 3, 0):
        attend(1, GROUPS - 1, (mx + d) % X)
        finish(1, d)

    def drain(group, _):
        sent(1, group)
        return 0

    lax.fori_loop(GROUPS - AHEAD, GROUPS, drain, 0)
    for d in range(1, X):
        norm_copy(0, d).wait_send()
        norm_copy(1, d).wait_send()
        wout_copy(d).wait_send()
        gate_copy(0, d).wait_send()
    output(1)
    for d in range(1, X):
        gate_copy(1, d).wait_send()


def local(cand_states, in_proj, out_proj, history, lengths, rank_users, recency_bias, score_weight):
    members_first = jnp.transpose(cand_states, (1, 0, 2))
    in_matrix = in_proj.reshape(D, 4 * HW)
    stored = history.reshape(history.shape[1:])
    smem = pl.BlockSpec(memory_space=pltpu.SMEM)
    vmem = pl.BlockSpec(memory_space=pltpu.VMEM)
    hbm = pl.BlockSpec(memory_space=pl.ANY)
    dma = pltpu.SemaphoreType.DMA
    out, scores = pl.pallas_call(
        kernel,
        out_shape=(
            jax.ShapeDtypeStruct((MEMBERS, ROWS, D), BF16),
            jax.ShapeDtypeStruct((MEMBERS, ROWS), F32),
        ),
        in_specs=[smem, smem, smem, vmem, hbm, hbm, hbm, hbm],
        out_specs=(vmem, vmem),
        scratch_shapes=[
            pltpu.VMEM(stored.shape, BF16),
            pltpu.VMEM((MEMBERS, CACHE, 2, EV, HW), BF16),
            pltpu.VMEM((MEMBERS, CACHE, 2, EV, HW), BF16),
            pltpu.VMEM((MEMBERS, ROWS, D), BF16),
            pltpu.VMEM((MEMBERS, X, ROWS, D), BF16),
            pltpu.VMEM((D, 4 * HW), BF16),
            pltpu.VMEM((X, HW, D), BF16),
            pltpu.VMEM((MEMBERS, 4, X * ROWS, HW), BF16),
            pltpu.VMEM((MEMBERS, HEADS_HERE, X * ROWS, HD), F32),
            pltpu.VMEM((MEMBERS, X, ROWS, HW), BF16),
            pltpu.VMEM((MEMBERS, X, ROWS, HW), BF16),
            pltpu.VMEM((MEMBERS, HEADS_HERE, GROUPS, 1, IN_GROUP * EV), F32),
            dma((4,)),
            dma((MEMBERS, CACHE, 2)),
            dma((MEMBERS, CACHE, 2)),
            dma((MEMBERS, X)),
            dma((MEMBERS, X)),
            dma((X,)),
            dma((X,)),
            dma((MEMBERS, X)),
            dma((MEMBERS, X)),
        ],
        compiler_params=pltpu.CompilerParams(
            collective_id=0, has_side_effects=True, vmem_limit_bytes=63 << 20
        ),
    )(
        lengths,
        rank_users,
        recency_bias,
        score_weight.reshape(1, D),
        members_first,
        in_matrix,
        out_proj,
        stored,
    )
    return jnp.transpose(out, (1, 0, 2)), scores.T


def solution(mesh):
    in_specs = (
        P("cand", "cache", None),
        P(None, None, "cand"),
        P("cand", None),
        P("cache", None, None, None, "cand"),
        P(),
        P(),
        P("cand", None),
        P(),
    )
    out_specs = (P("cand", "cache", None), P("cand", "cache"))
    return jax.shard_map(local, mesh=mesh, in_specs=in_specs, out_specs=out_specs, check_vma=False)
```

```python
import functools

import jax
import jax.numpy as jnp
from jax import lax
from jax.experimental import pallas as pl
from jax.experimental.pallas import tpu as pltpu
from jax.sharding import PartitionSpec as P

EPSILON = 1e-06
MESH = pl.DeviceIdType.MESH
BF16, F32 = jnp.bfloat16, jnp.float32

X = 4
SIDE = 4
CACHE = 2 * SIDE * SIDE
MEMBERS = 2
HEADS_HERE, HD = 2, 128
HW = HEADS_HERE * HD
ROWS = 256
D = 1024
EV = 128
GROUPS, IN_GROUP = 8, 4
BUCKETS = 14
AHEAD = 6
BIAS_LANES = 16
FAR = 1 << 30
MASKED = -1e30


def silu(x):
    half = x * 0.5
    return half + half * jnp.tanh(half)


def kernel(
    lengths_ref,
    users_ref,
    recency_ref,
    weight_ref,
    cand_hbm,
    win_hbm,
    wout_hbm,
    hist_hbm,
    out_ref,
    scores_ref,
    hist_v,
    send_v,
    arr_v,
    cand_v,
    norm_v,
    win_v,
    wout_v,
    proj_v,
    tot_v,
    gated_v,
    spread_v,
    onehot_v,
    bias_v,
    local_sem,
    hist_ss,
    hist_rs,
    norm_ss,
    norm_rs,
    wout_ss,
    wout_rs,
    gate_ss,
    gate_rs,
):
    me, mx = lax.axis_index("cache"), lax.axis_index("cand")
    my_y, my_z, my_core = me // (2 * SIDE), (me // 2) % SIDE, me % 2
    scale = HD ** (-0.5)

    def cache_at(group, b, sign):
        a, dc = group // 2, group % 2
        ny = (my_y + sign * b + SIDE) % SIDE
        nz = (my_z + sign * ((a + b) % SIDE) + SIDE) % SIDE
        nc = (my_core + dc) % 2
        return (ny * SIDE + nz) * 2 + nc

    def hist_copy(m, group, b, kv):
        slot = group * IN_GROUP + b
        return pltpu.make_async_remote_copy(
            src_ref=send_v.at[m, slot, kv],
            dst_ref=arr_v.at[m, slot, kv],
            send_sem=hist_ss.at[m, slot, kv],
            recv_sem=hist_rs.at[m, slot, kv],
            device_id={"cache": cache_at(group, b, 1), "cand": mx},
            device_id_type=MESH,
        )

    def norm_copy(m, d):
        return pltpu.make_async_remote_copy(
            src_ref=norm_v.at[m, mx],
            dst_ref=norm_v.at[m, mx],
            send_sem=norm_ss.at[m, d],
            recv_sem=norm_rs.at[m, d],
            device_id={"cache": me, "cand": (mx + d) % X},
            device_id_type=MESH,
        )

    def wout_copy(d):
        return pltpu.make_async_remote_copy(
            src_ref=wout_v.at[mx],
            dst_ref=wout_v.at[mx],
            send_sem=wout_ss.at[d],
            recv_sem=wout_rs.at[d],
            device_id={"cache": me, "cand": (mx + d) % X},
            device_id_type=MESH,
        )

    def gate_copy(m, d):
        return pltpu.make_async_remote_copy(
            src_ref=gated_v.at[m, (mx + d) % X],
            dst_ref=spread_v.at[m, mx],
            send_sem=gate_ss.at[m, d],
            recv_sem=gate_rs.at[m, d],
            device_id={"cache": me, "cand": (mx + d) % X},
            device_id_type=MESH,
        )

    cand_in = pltpu.make_async_copy(cand_hbm, cand_v, local_sem.at[0])
    hist_in = pltpu.make_async_copy(hist_hbm, hist_v, local_sem.at[1])
    win_in = pltpu.make_async_copy(win_hbm, win_v, local_sem.at[2])
    wout_in = pltpu.make_async_copy(wout_hbm, wout_v.at[mx], local_sem.at[3])
    cand_in.start()
    hist_in.start()
    win_in.start()
    wout_in.start()

    barrier = pltpu.get_barrier_semaphore()

    def greet(j, _):
        pl.semaphore_signal(
            barrier,
            inc=1,
            device_id={"cache": (me + j) % CACHE, "cand": mx},
            device_id_type=MESH,
        )
        return 0

    lax.fori_loop(1, CACHE, greet, 0)
    for d in range(1, X):
        pl.semaphore_signal(
            barrier, inc=1, device_id={"cache": me, "cand": (mx + d) % X}, device_id_type=MESH
        )

    cand_in.wait()
    TILE = 32

    def normalize(i, _):
        m, r = i // (ROWS // TILE), i % (ROWS // TILE)
        rows = pl.ds(pl.multiple_of(r * TILE, TILE), TILE)
        x = cand_v[m, rows, :].astype(F32)
        inv = lax.rsqrt(jnp.mean(x * x, axis=-1, keepdims=True) + EPSILON)
        norm_v[m, mx, rows, :] = (x * inv).astype(BF16)
        return 0

    lax.fori_loop(0, MEMBERS * (ROWS // TILE), normalize, 0)
    pl.semaphore_wait(barrier, CACHE - 1 + X - 1)
    for d in (2, 1, 3):
        norm_copy(0, d).start()
    hist_in.wait()

    def gather(m, group):
        for b in range(IN_GROUP):
            user = users_ref[MEMBERS * cache_at(group, b, 1) + m]
            block = hist_v[user]
            slot = group * IN_GROUP + b
            if b == 0:
                own = group == 0

                @pl.when(own)
                def _():
                    arr_v[m, slot] = block

                @pl.when(jnp.logical_not(own))
                def _():
                    send_v[m, slot] = block
            else:
                send_v[m, slot] = block

    def send(m, group):
        for kv in range(2):
            for b in range(IN_GROUP):
                if b == 0:

                    @pl.when(group > 0)
                    def _():
                        hist_copy(m, group, b, kv).start()
                else:
                    hist_copy(m, group, b, kv).start()

    gather(0, 0)

    def gather_and_send(group, _):
        @pl.when(group < GROUPS - 1)
        def _():
            gather(0, group + 1)

        send(0, group)
        return 0

    lax.fori_loop(0, GROUPS, gather_and_send, 0)
    for d in (2, 1, 3):
        norm_copy(1, d).start()
    wout_in.wait()
    for d in (2, 1, 3):
        wout_copy(d).start()

    def gather_next(group, _):
        gather(1, group)
        return 0

    lax.fori_loop(0, GROUPS, gather_next, 0)

    lane = lax.broadcasted_iota(jnp.int32, (1, HD), 1)
    bucket = jnp.where(lane < 3 * BIAS_LANES, lane % BIAS_LANES, 0)
    low = jnp.full((1, HD), FAR, jnp.int32)
    high = jnp.full((1, HD), FAR, jnp.int32)
    for k in range(1, BUCKETS):
        low = jnp.where(bucket == k, 2 ** (k - 1), low)
        high = jnp.where(bucket == k, FAR if k == BUCKETS - 1 else 2**k, high)
    low = jnp.where(bucket == BUCKETS, -FAR, low)
    high = jnp.where(bucket == BUCKETS, 1, high)
    for h in range(HEADS_HERE):
        bias = jnp.zeros((1, HD), F32)
        for k in range(1, BUCKETS):
            bias = jnp.where(bucket == k, recency_ref[h, k] * 0.5, bias)
        first = bias.astype(BF16).astype(F32)
        second = (bias - first).astype(BF16).astype(F32)
        third = bias - first - second
        row = jnp.where(lane < 2 * BIAS_LANES, second, third)
        row = jnp.where(lane < BIAS_LANES, first, row)
        row = jnp.where(lane == BUCKETS, MASKED, row)
        bias_v[h] = jnp.broadcast_to(row, (ROWS, HD)).astype(BF16)
    event = lax.broadcasted_iota(jnp.int32, (EV, HD), 0)

    def buckets_of(i, _):
        m, group = i // GROUPS, i % GROUPS
        user = users_ref[MEMBERS * me + m]
        length = lengths_ref[user]
        for b in range(IN_GROUP):
            shard = cache_at(group, b, -1)
            start = lax.rem(shard - user + 4 * CACHE, CACHE) * EV
            distance = (length - start) - event
            hit = (distance >= low) & (distance < high)
            onehot_v[m, group * IN_GROUP + b] = jnp.where(hit, 1.0, 0.0).astype(BF16)
        return 0

    lax.fori_loop(0, MEMBERS * GROUPS, buckets_of, 0)
    win_in.wait()

    def project(m):
        def from_source(d, _):
            @pl.when(d > 0)
            def _():
                norm_copy(m, d).wait_recv()

            source = (mx - d + X) % X

            def one_kind(kind, _):
                columns = pl.ds(pl.multiple_of(kind * HW, HW), HW)
                product = jnp.dot(
                    norm_v[m, source], win_v[:, columns], preferred_element_type=F32
                )
                rows = pl.ds(pl.multiple_of(source * ROWS, ROWS), ROWS)
                factor = jnp.where(kind == 2, 0.5 * scale, 1.0)
                proj_v[m, kind, rows, :] = (silu(product) * factor).astype(BF16)
                return 0

            lax.fori_loop(0, 4, one_kind, 0)
            return 0

        lax.fori_loop(0, X, from_source, 0)

        def own_term(t, _):
            rows = pl.ds(pl.multiple_of(t * ROWS, ROWS), ROWS)
            for h in range(HEADS_HERE):
                cols = slice(h * HD, (h + 1) * HD)
                values = proj_v[m, 1, rows, cols].astype(F32)
                queries = proj_v[m, 2, rows, cols].astype(F32)
                keys = proj_v[m, 3, rows, cols].astype(F32)
                half = jnp.sum(queries * keys, axis=-1, keepdims=True) + recency_ref[h, 0] * 0.5
                tot_v[m, h, rows, :] = (half + half * jnp.tanh(half)) * values
            return 0

        lax.fori_loop(0, X, own_term, 0)

    def arrived(m, group):
        for b in range(IN_GROUP):
            for kv in range(2):
                if b == 0:

                    @pl.when(group > 0)
                    def _():
                        hist_copy(m, group, b, kv).wait_recv()
                else:
                    hist_copy(m, group, b, kv).wait_recv()

    def sent(m, group):
        for b in range(IN_GROUP):
            for kv in range(2):
                if b == 0:

                    @pl.when(group > 0)
                    def _():
                        hist_copy(m, group, b, kv).wait_send()
                else:
                    hist_copy(m, group, b, kv).wait_send()

    def attend(m, group, t):
        rows = pl.ds(pl.multiple_of(t * ROWS, ROWS), ROWS)
        slots = pl.ds(group * IN_GROUP, IN_GROUP)
        for h in range(HEADS_HERE):
            cols = slice(h * HD, (h + 1) * HD)
            keys = arr_v[m, slots, 0, :, cols].reshape(IN_GROUP * EV, HD)
            values = arr_v[m, slots, 1, :, cols].reshape(IN_GROUP * EV, HD)
            near = onehot_v[m, slots].reshape(IN_GROUP * EV, HD)
            half = lax.dot_general(
                jnp.concatenate([proj_v[m, 2, rows, cols], bias_v[h]], axis=1),
                jnp.concatenate([keys, near], axis=1),
                (((1,), (1,)), ((), ())),
                preferred_element_type=F32,
            )
            weights = (half + half * jnp.tanh(half)).astype(BF16)
            tot_v[m, h, rows, :] += jnp.dot(weights, values, preferred_element_type=F32)

    def finish(m, d):
        t = (mx + d) % X
        rows = pl.ds(pl.multiple_of(t * ROWS, ROWS), ROWS)
        for h in range(HEADS_HERE):
            cols = slice(h * HD, (h + 1) * HD)
            total = tot_v[m, h, rows, :]
            inv = lax.rsqrt(jnp.mean(total * total, axis=-1, keepdims=True) + EPSILON)
            value = (total * inv * proj_v[m, 0, rows, cols].astype(F32)).astype(BF16)
            if d == 0:
                spread_v[m, mx, :, cols] = value
            else:
                gated_v[m, t, :, cols] = value
        if d != 0:
            gate_copy(m, d).start()

    def attend_groups(m, first, last):
        def step(group, _):
            arrived(m, group)
            if m == 0:
                sent(0, group)

                @pl.when(group + AHEAD >= GROUPS)
                def _():
                    send(1, group + AHEAD - GROUPS)
            else:

                @pl.when(group + AHEAD < GROUPS)
                def _():
                    sent(1, group)
                    send(1, group + AHEAD)

            def tile(t, _):
                attend(m, group, t)
                return 0

            lax.fori_loop(0, X, tile, 0)
            return 0

        lax.fori_loop(first, last, step, 0)

    def output(m):
        for d in range(1, X):
            gate_copy(m, d).wait_recv()
        partial = jnp.zeros((ROWS, HD), F32)
        wide = 256
        for c in range(D // wide):
            cols = slice(c * wide, (c + 1) * wide)
            total = cand_v[m, :, cols].astype(F32)
            for s in range(X):
                total += jnp.dot(spread_v[m, s], wout_v[s, :, cols], preferred_element_type=F32)
            out_ref[m, :, cols] = total.astype(BF16)
            weighted = total * weight_ref[:, cols]
            for k in range(wide // HD):
                partial += weighted[:, k * HD : (k + 1) * HD]
        scores_ref[m : m + 1, :] = jnp.sum(partial.T, axis=0, keepdims=True)

    project(0)
    attend_groups(0, 0, GROUPS)
    for d in (2, 1, 3, 0):
        finish(0, d)
    project(1)
    attend_groups(1, 0, GROUPS // 2)
    for d in range(1, X):
        wout_copy(d).wait_recv()
    output(0)
    attend_groups(1, GROUPS // 2, GROUPS - 1)
    arrived(1, GROUPS - 1)
    for d in (2, 1, 3, 0):
        attend(1, GROUPS - 1, (mx + d) % X)
        finish(1, d)

    def drain(group, _):
        sent(1, group)
        return 0

    lax.fori_loop(GROUPS - AHEAD, GROUPS, drain, 0)
    for d in range(1, X):
        norm_copy(0, d).wait_send()
        norm_copy(1, d).wait_send()
        wout_copy(d).wait_send()
        gate_copy(0, d).wait_send()
    output(1)
    for d in range(1, X):
        gate_copy(1, d).wait_send()


def local(cand_states, in_proj, out_proj, history, lengths, rank_users, recency_bias, score_weight):
    members_first = jnp.transpose(cand_states, (1, 0, 2))
    in_matrix = in_proj.reshape(D, 4 * HW)
    stored = history.reshape(history.shape[1:])
    smem = pl.BlockSpec(memory_space=pltpu.SMEM)
    vmem = pl.BlockSpec(memory_space=pltpu.VMEM)
    hbm = pl.BlockSpec(memory_space=pl.ANY)
    dma = pltpu.SemaphoreType.DMA
    out, scores = pl.pallas_call(
        kernel,
        out_shape=(
            jax.ShapeDtypeStruct((MEMBERS, ROWS, D), BF16),
            jax.ShapeDtypeStruct((MEMBERS, ROWS), F32),
        ),
        in_specs=[smem, smem, smem, vmem, hbm, hbm, hbm, hbm],
        out_specs=(vmem, vmem),
        scratch_shapes=[
            pltpu.VMEM(stored.shape, BF16),
            pltpu.VMEM((MEMBERS, CACHE, 2, EV, HW), BF16),
            pltpu.VMEM((MEMBERS, CACHE, 2, EV, HW), BF16),
            pltpu.VMEM((MEMBERS, ROWS, D), BF16),
            pltpu.VMEM((MEMBERS, X, ROWS, D), BF16),
            pltpu.VMEM((D, 4 * HW), BF16),
            pltpu.VMEM((X, HW, D), BF16),
            pltpu.VMEM((MEMBERS, 4, X * ROWS, HW), BF16),
            pltpu.VMEM((MEMBERS, HEADS_HERE, X * ROWS, HD), F32),
            pltpu.VMEM((MEMBERS, X, ROWS, HW), BF16),
            pltpu.VMEM((MEMBERS, X, ROWS, HW), BF16),
            pltpu.VMEM((MEMBERS, CACHE, EV, HD), BF16),
            pltpu.VMEM((HEADS_HERE, ROWS, HD), BF16),
            dma((4,)),
            dma((MEMBERS, CACHE, 2)),
            dma((MEMBERS, CACHE, 2)),
            dma((MEMBERS, X)),
            dma((MEMBERS, X)),
            dma((X,)),
            dma((X,)),
            dma((MEMBERS, X)),
            dma((MEMBERS, X)),
        ],
        compiler_params=pltpu.CompilerParams(
            collective_id=0, has_side_effects=True, vmem_limit_bytes=63 << 20
        ),
    )(
        lengths,
        rank_users,
        recency_bias,
        score_weight.reshape(1, D),
        members_first,
        in_matrix,
        out_proj,
        stored,
    )
    return jnp.transpose(out, (1, 0, 2)), scores.T


def solution(mesh):
    in_specs = (
        P("cand", "cache", None),
        P(None, None, "cand"),
        P("cand", None),
        P("cache", None, None, None, "cand"),
        P(),
        P(),
        P("cand", None),
        P(),
    )
    out_specs = (P("cand", "cache", None), P("cand", "cache"))
    return jax.shard_map(local, mesh=mesh, in_specs=in_specs, out_specs=out_specs, check_vma=False)
```

```python
import functools

import jax
import jax.numpy as jnp
from jax import lax
from jax.experimental import pallas as pl
from jax.experimental.pallas import tpu as pltpu
from jax.sharding import PartitionSpec as P

EPSILON = 1e-06
MESH = pl.DeviceIdType.MESH
BF16, F32 = jnp.bfloat16, jnp.float32

X = 4
SIDE = 4
CACHE = 2 * SIDE * SIDE
MEMBERS = 2
HEADS_HERE, HD = 2, 128
HW = HEADS_HERE * HD
ROWS = 256
D = 1024
EV = 128
GROUPS, IN_GROUP = 8, 4
BUCKETS = 14
AHEAD = 6
MASKED = -1e30


def silu(x):
    half = x * 0.5
    return half + half * jnp.tanh(half)


def kernel(
    lengths_ref,
    users_ref,
    recency_ref,
    weight_ref,
    cand_hbm,
    win_hbm,
    wout_hbm,
    hist_hbm,
    out_ref,
    scores_ref,
    hist_v,
    send_v,
    arr_v,
    cand_v,
    norm_v,
    win_v,
    wout_v,
    proj_v,
    tot_v,
    gated_v,
    spread_v,
    bias_v,
    local_sem,
    hist_ss,
    hist_rs,
    norm_ss,
    norm_rs,
    wout_ss,
    wout_rs,
    gate_ss,
    gate_rs,
):
    me, mx = lax.axis_index("cache"), lax.axis_index("cand")
    my_y, my_z, my_core = me // (2 * SIDE), (me // 2) % SIDE, me % 2
    scale = HD ** (-0.5)

    def cache_at(group, b, sign):
        a, dc = group // 2, group % 2
        ny = (my_y + sign * b + SIDE) % SIDE
        nz = (my_z + sign * ((a + b) % SIDE) + SIDE) % SIDE
        nc = (my_core + dc) % 2
        return (ny * SIDE + nz) * 2 + nc

    def hist_copy(m, group, b, kv):
        slot = group * IN_GROUP + b
        return pltpu.make_async_remote_copy(
            src_ref=send_v.at[m, slot, kv],
            dst_ref=arr_v.at[m, slot, kv],
            send_sem=hist_ss.at[m, slot, kv],
            recv_sem=hist_rs.at[m, slot, kv],
            device_id={"cache": cache_at(group, b, 1), "cand": mx},
            device_id_type=MESH,
        )

    def norm_copy(m, d):
        return pltpu.make_async_remote_copy(
            src_ref=norm_v.at[m, mx],
            dst_ref=norm_v.at[m, mx],
            send_sem=norm_ss.at[m, d],
            recv_sem=norm_rs.at[m, d],
            device_id={"cache": me, "cand": (mx + d) % X},
            device_id_type=MESH,
        )

    def wout_copy(d):
        return pltpu.make_async_remote_copy(
            src_ref=wout_v.at[mx],
            dst_ref=wout_v.at[mx],
            send_sem=wout_ss.at[d],
            recv_sem=wout_rs.at[d],
            device_id={"cache": me, "cand": (mx + d) % X},
            device_id_type=MESH,
        )

    def gate_copy(m, d):
        return pltpu.make_async_remote_copy(
            src_ref=gated_v.at[m, (mx + d) % X],
            dst_ref=spread_v.at[m, mx],
            send_sem=gate_ss.at[m, d],
            recv_sem=gate_rs.at[m, d],
            device_id={"cache": me, "cand": (mx + d) % X},
            device_id_type=MESH,
        )

    cand_in = pltpu.make_async_copy(cand_hbm, cand_v, local_sem.at[0])
    hist_in = pltpu.make_async_copy(hist_hbm, hist_v, local_sem.at[1])
    win_in = pltpu.make_async_copy(win_hbm, win_v, local_sem.at[2])
    wout_in = pltpu.make_async_copy(wout_hbm, wout_v.at[mx], local_sem.at[3])
    hist_in.start()
    cand_in.start()
    win_in.start()
    wout_in.start()

    barrier = pltpu.get_barrier_semaphore()

    def greet(j, _):
        pl.semaphore_signal(
            barrier,
            inc=1,
            device_id={"cache": (me + j) % CACHE, "cand": mx},
            device_id_type=MESH,
        )
        return 0

    lax.fori_loop(1, CACHE, greet, 0)
    for d in range(1, X):
        pl.semaphore_signal(
            barrier, inc=1, device_id={"cache": me, "cand": (mx + d) % X}, device_id_type=MESH
        )

    pl.semaphore_wait(barrier, CACHE - 1 + X - 1)
    hist_in.wait()

    def gather(m, group):
        for b in range(IN_GROUP):
            user = users_ref[MEMBERS * cache_at(group, b, 1) + m]
            block = hist_v[user]
            slot = group * IN_GROUP + b
            if b == 0:
                own = group == 0

                @pl.when(own)
                def _():
                    arr_v[m, slot] = block

                @pl.when(jnp.logical_not(own))
                def _():
                    send_v[m, slot] = block
            else:
                send_v[m, slot] = block

    def send(m, group):
        for kv in range(2):
            for b in range(IN_GROUP):
                if b == 0:

                    @pl.when(group > 0)
                    def _():
                        hist_copy(m, group, b, kv).start()
                else:
                    hist_copy(m, group, b, kv).start()

    gather(0, 0)

    def gather_and_send(group, _):
        @pl.when(group < GROUPS - 1)
        def _():
            gather(0, group + 1)

        send(0, group)
        return 0

    lax.fori_loop(0, GROUPS, gather_and_send, 0)
    cand_in.wait()
    TILE = 32

    def normalize(i, _):
        m, r = i // (ROWS // TILE), i % (ROWS // TILE)
        rows = pl.ds(pl.multiple_of(r * TILE, TILE), TILE)
        x = cand_v[m, rows, :].astype(F32)
        inv = lax.rsqrt(jnp.mean(x * x, axis=-1, keepdims=True) + EPSILON)
        norm_v[m, mx, rows, :] = (x * inv).astype(BF16)
        return 0

    lax.fori_loop(0, MEMBERS * (ROWS // TILE), normalize, 0)
    for m in range(MEMBERS):
        for d in (2, 1, 3):
            norm_copy(m, d).start()
    wout_in.wait()
    for d in (2, 1, 3):
        wout_copy(d).start()

    def gather_next(group, _):
        gather(1, group)
        return 0

    lax.fori_loop(0, GROUPS, gather_next, 0)

    lanes = lax.broadcasted_iota(jnp.int32, (1, EV), 1)

    def bias_of(i, _):
        m, group = i // GROUPS, i % GROUPS
        user = users_ref[MEMBERS * me + m]
        length = lengths_ref[user]
        for b in range(IN_GROUP):
            shard = cache_at(group, b, -1)
            position = lax.rem(shard - user + 4 * CACHE, CACHE) * EV + lanes
            distance = jnp.maximum(length - position, 0)
            usable = position < length
            for h in range(HEADS_HERE):
                bias = jnp.full((1, EV), recency_ref[h, 0], F32)
                for k in range(BUCKETS - 1):
                    bias = jnp.where(distance >= 2**k, recency_ref[h, k + 1], bias)
                bias = jnp.where(usable, bias * 0.5, MASKED)
                bias_v[m, h, group, :, b * EV : (b + 1) * EV] = bias
        return 0

    lax.fori_loop(0, MEMBERS * GROUPS, bias_of, 0)
    win_in.wait()

    def project(m):
        def from_source(d, _):
            @pl.when(d > 0)
            def _():
                norm_copy(m, d).wait_recv()

            source = (mx - d + X) % X

            def one_kind(kind, _):
                columns = pl.ds(pl.multiple_of(kind * HW, HW), HW)
                product = jnp.dot(
                    norm_v[m, source], win_v[:, columns], preferred_element_type=F32
                )
                rows = pl.ds(pl.multiple_of(source * ROWS, ROWS), ROWS)
                proj_v[m, kind, rows, :] = silu(product).astype(BF16)
                return 0

            lax.fori_loop(0, 4, one_kind, 0)
            return 0

        lax.fori_loop(0, X, from_source, 0)

        def own_term(t, _):
            rows = pl.ds(pl.multiple_of(t * ROWS, ROWS), ROWS)
            for h in range(HEADS_HERE):
                cols = slice(h * HD, (h + 1) * HD)
                values = proj_v[m, 1, rows, cols].astype(F32)
                queries = proj_v[m, 2, rows, cols].astype(F32)
                keys = proj_v[m, 3, rows, cols].astype(F32)
                score = jnp.sum(queries * keys, axis=-1, keepdims=True) * scale + recency_ref[h, 0]
                tot_v[m, h, rows, :] = silu(score) * values
            return 0

        lax.fori_loop(0, X, own_term, 0)

    def arrived(m, group):
        for b in range(IN_GROUP):
            for kv in range(2):
                if b == 0:

                    @pl.when(group > 0)
                    def _():
                        hist_copy(m, group, b, kv).wait_recv()
                else:
                    hist_copy(m, group, b, kv).wait_recv()

    def sent(m, group):
        for b in range(IN_GROUP):
            for kv in range(2):
                if b == 0:

                    @pl.when(group > 0)
                    def _():
                        hist_copy(m, group, b, kv).wait_send()
                else:
                    hist_copy(m, group, b, kv).wait_send()

    def attend(m, group, t):
        rows = pl.ds(pl.multiple_of(t * ROWS, ROWS), ROWS)
        slots = pl.ds(group * IN_GROUP, IN_GROUP)
        for h in range(HEADS_HERE):
            cols = slice(h * HD, (h + 1) * HD)
            keys = arr_v[m, slots, 0, :, cols].reshape(IN_GROUP * EV, HD)
            values = arr_v[m, slots, 1, :, cols].reshape(IN_GROUP * EV, HD)
            scores = lax.dot_general(
                proj_v[m, 2, rows, cols],
                keys,
                (((1,), (1,)), ((), ())),
                preferred_element_type=F32,
            )
            half = scores * (0.5 * scale) + bias_v[m, h, group]
            weights = (half + half * jnp.tanh(half)).astype(BF16)
            tot_v[m, h, rows, :] += jnp.dot(weights, values, preferred_element_type=F32)

    def finish(m, d):
        t = (mx + d) % X
        rows = pl.ds(pl.multiple_of(t * ROWS, ROWS), ROWS)
        for h in range(HEADS_HERE):
            cols = slice(h * HD, (h + 1) * HD)
            total = tot_v[m, h, rows, :]
            inv = lax.rsqrt(jnp.mean(total * total, axis=-1, keepdims=True) + EPSILON)
            value = (total * inv * proj_v[m, 0, rows, cols].astype(F32)).astype(BF16)
            if d == 0:
                spread_v[m, mx, :, cols] = value
            else:
                gated_v[m, t, :, cols] = value
        if d != 0:
            gate_copy(m, d).start()

    def attend_groups(m, first, last):
        def step(group, _):
            arrived(m, group)
            if m == 0:
                sent(0, group)

                @pl.when(group + AHEAD >= GROUPS)
                def _():
                    send(1, group + AHEAD - GROUPS)
            else:

                @pl.when(group + AHEAD < GROUPS)
                def _():
                    sent(1, group)
                    send(1, group + AHEAD)

            def tile(t, _):
                attend(m, group, t)
                return 0

            lax.fori_loop(0, X, tile, 0)
            return 0

        lax.fori_loop(first, last, step, 0)

    def output(m):
        for d in range(1, X):
            gate_copy(m, d).wait_recv()
        partial = jnp.zeros((ROWS, HD), F32)
        wide = 256
        for c in range(D // wide):
            cols = slice(c * wide, (c + 1) * wide)
            total = cand_v[m, :, cols].astype(F32)
            for s in range(X):
                total += jnp.dot(spread_v[m, s], wout_v[s, :, cols], preferred_element_type=F32)
            out_ref[m, :, cols] = total.astype(BF16)
            weighted = total * weight_ref[:, cols]
            for k in range(wide // HD):
                partial += weighted[:, k * HD : (k + 1) * HD]
        scores_ref[m : m + 1, :] = jnp.sum(partial.T, axis=0, keepdims=True)

    project(0)
    attend_groups(0, 0, GROUPS)
    for d in (2, 1, 3, 0):
        finish(0, d)
    project(1)
    attend_groups(1, 0, GROUPS // 2)
    for d in range(1, X):
        wout_copy(d).wait_recv()
    output(0)
    attend_groups(1, GROUPS // 2, GROUPS - 1)
    arrived(1, GROUPS - 1)
    for d in (2, 1, 3, 0):
        attend(1, GROUPS - 1, (mx + d) % X)
        finish(1, d)

    def drain(group, _):
        sent(1, group)
        return 0

    lax.fori_loop(GROUPS - AHEAD, GROUPS, drain, 0)
    for d in range(1, X):
        norm_copy(0, d).wait_send()
        norm_copy(1, d).wait_send()
        wout_copy(d).wait_send()
        gate_copy(0, d).wait_send()
    output(1)
    for d in range(1, X):
        gate_copy(1, d).wait_send()


def local(cand_states, in_proj, out_proj, history, lengths, rank_users, recency_bias, score_weight):
    members_first = jnp.transpose(cand_states, (1, 0, 2))
    in_matrix = in_proj.reshape(D, 4 * HW)
    stored = history.reshape(history.shape[1:])
    smem = pl.BlockSpec(memory_space=pltpu.SMEM)
    vmem = pl.BlockSpec(memory_space=pltpu.VMEM)
    hbm = pl.BlockSpec(memory_space=pl.ANY)
    dma = pltpu.SemaphoreType.DMA
    out, scores = pl.pallas_call(
        kernel,
        out_shape=(
            jax.ShapeDtypeStruct((MEMBERS, ROWS, D), BF16),
            jax.ShapeDtypeStruct((MEMBERS, ROWS), F32),
        ),
        in_specs=[smem, smem, smem, vmem, hbm, hbm, hbm, hbm],
        out_specs=(vmem, vmem),
        scratch_shapes=[
            pltpu.VMEM(stored.shape, BF16),
            pltpu.VMEM((MEMBERS, CACHE, 2, EV, HW), BF16),
            pltpu.VMEM((MEMBERS, CACHE, 2, EV, HW), BF16),
            pltpu.VMEM((MEMBERS, ROWS, D), BF16),
            pltpu.VMEM((MEMBERS, X, ROWS, D), BF16),
            pltpu.VMEM((D, 4 * HW), BF16),
            pltpu.VMEM((X, HW, D), BF16),
            pltpu.VMEM((MEMBERS, 4, X * ROWS, HW), BF16),
            pltpu.VMEM((MEMBERS, HEADS_HERE, X * ROWS, HD), F32),
            pltpu.VMEM((MEMBERS, X, ROWS, HW), BF16),
            pltpu.VMEM((MEMBERS, X, ROWS, HW), BF16),
            pltpu.VMEM((MEMBERS, HEADS_HERE, GROUPS, 1, IN_GROUP * EV), F32),
            dma((4,)),
            dma((MEMBERS, CACHE, 2)),
            dma((MEMBERS, CACHE, 2)),
            dma((MEMBERS, X)),
            dma((MEMBERS, X)),
            dma((X,)),
            dma((X,)),
            dma((MEMBERS, X)),
            dma((MEMBERS, X)),
        ],
        compiler_params=pltpu.CompilerParams(
            collective_id=0, has_side_effects=True, vmem_limit_bytes=63 << 20
        ),
    )(
        lengths,
        rank_users,
        recency_bias,
        score_weight.reshape(1, D),
        members_first,
        in_matrix,
        out_proj,
        stored,
    )
    return jnp.transpose(out, (1, 0, 2)), scores.T


def solution(mesh):
    in_specs = (
        P("cand", "cache", None),
        P(None, None, "cand"),
        P("cand", None),
        P("cache", None, None, None, "cand"),
        P(),
        P(),
        P("cand", None),
        P(),
    )
    out_specs = (P("cand", "cache", None), P("cand", "cache"))
    return jax.shard_map(local, mesh=mesh, in_specs=in_specs, out_specs=out_specs, check_vma=False)
```
